256 devices in a mesh: ctx: 128 (over x_lo, y, z, core), tp: 2 (over x_hi).
Axes of the slice: x: 4 (x_hi: 2, x_lo: 2; x = x_hi * 2 + x_lo), y: 4, z: 8, core: 2. Of those that a mesh axis runs over, the one named last changes fastest.
Arguments:
- queries: bfloat16 [32768, 2048], P('ctx', 'tp'), may hold values from -5 to 5
- keys: bfloat16 [32768, 256], P('ctx', 'tp'), may hold values from -5 to 5
- values: bfloat16 [32768, 256], P('ctx', 'tp'), may hold values from -6 to 6
- out_weight: bfloat16 [2048, 4096], P('tp'), may hold values from -0.125 to 0.125
- cotangent: bfloat16 [32768, 4096], P('ctx', 'tp'), may hold values from -6 to 6
- doc_lengths: int32 [64], replicated, may hold values from 1 to 2048, 32768 in all
Outputs:
- mixed_out: bfloat16 [32768, 4096], P('ctx', 'tp')
- query_grad: bfloat16 [32768, 2048], P('ctx', 'tp')
- keys_gradient: bfloat16 [32768, 256], P('ctx', 'tp')
- values_gradient: bfloat16 [32768, 256], P('ctx', 'tp')
The draws below stay inside these ranges and needn't reach their ends.
Inputs may be any that keep to these rules, and one draw needn't show every extreme that they name: `doc_lengths`: document lengths in order along the packed sequence; they sum to 32768 and the longest is exactly 2048.
All inputs are finite; a program needn't handle non-finite values.
Results may differ from the reference program's by a relative error of at most 0.022.
Values may be sent and summed in bfloat16 or wider, within the bound.
A program may use at most 192 MiB of HBM per device.

```python
import math
import jax
import jax.numpy as jnp
import numpy as np
from jax import lax

D = 4096
QUERY_HEADS = 16
KEY_VALUE_HEADS = 2
HEAD_WIDTH = 128
SHARD_TOKENS = 256
REACH = 8
PACKED_TOKENS = 32768
DOC_MOST = 2048
DOCS = 64


def draw_queries(key, part):
    local_keys = jax.random.fold_in(key, 11)
    sampled_inputs = jax.random.truncated_normal(local_keys, -4.0, 4.0, (PACKED_TOKENS, QUERY_HEADS, HEAD_WIDTH), jnp.float32)
    return sampled_inputs.reshape(PACKED_TOKENS, QUERY_HEADS * HEAD_WIDTH).astype(jnp.bfloat16)


def draw_keys(key, part):
    local_keys = jax.random.fold_in(key, 13)
    sampled_inputs = jax.random.truncated_normal(local_keys, -4.0, 4.0, (PACKED_TOKENS, KEY_VALUE_HEADS, HEAD_WIDTH), jnp.float32)
    return sampled_inputs.reshape(PACKED_TOKENS, KEY_VALUE_HEADS * HEAD_WIDTH).astype(jnp.bfloat16)


def level_of(own_key, shape, shards, low, top_value):
    level = 1.0
    for dim, blocks in shards:
        heights = jax.random.uniform(jax.random.fold_in(jax.random.fold_in(own_key, 6), dim), (blocks,), jnp.float32, low / len(shards), top_value / len(shards))
        level = level * jnp.repeat(jnp.exp(heights), shape[dim] // blocks).reshape((-1,) + (1,) * (len(shape) - 1 - dim))
    return level


def profile(count, total, reach, slope):
    loads = [(1 << 20) // math.isqrt(grade ** slope) + 1 for grade in range(2, count + 1)]
    rest, counts = total - reach - (count - 1), [1] * (count - 1)
    while rest > 0:
        movable = [i for i in range(count - 1) if counts[i] < reach]
        whole, remaining = sum([loads[i] for i in movable]), rest
        for i in movable:
            addition = min(reach - counts[i], max(1, remaining * loads[i] // whole), rest)
            counts[i] = counts[i] + addition
            rest = rest - addition
    return np.array([reach] + counts)


def uneven(stream_key, number_of, total, limit, lean):
    if number_of == 2:
        one = jax.random.randint(stream_key, (), max(1, total - limit), min(limit, total - 1) + 1)
        return jnp.stack([one, total - one])
    tallies = jnp.asarray(profile(number_of, total, limit, lean), jnp.int32)
    twos = (number_of - 1) // 2
    donor, receiver = tallies[1:1 + 2 * twos:2], tallies[2:2 + 2 * twos:2]
    margin = jnp.minimum(donor - 1, limit - receiver)
    moved = jax.random.randint(jax.random.fold_in(stream_key, 1), (twos,), 0, 1 << 20) % (margin + 1)
    tallies = tallies.at[1:1 + 2 * twos:2].set(donor - moved).at[2:2 + 2 * twos:2].set(receiver + moved)
    return tallies[jax.random.permutation(jax.random.fold_in(stream_key, 2), number_of)]


def gaussian(stream_key, shape, deviation, most, cuts=(), kind=jnp.bfloat16):
    entries = jax.random.normal(stream_key, shape, jnp.float32) * deviation
    if len(cuts) > 0:
        entries = level_of(stream_key, shape, cuts, -0.22, 0.18) * entries
    return jnp.clip(entries, min=-most, max=most).astype(kind)


def setup_inputs(seed: int = 0) -> dict:
    key_list = jax.random.split(jax.random.key(seed), 7)
    return {
        "queries": draw_queries(jax.random.fold_in(key_list[6], 71), 0),
        "keys": draw_keys(jax.random.fold_in(key_list[6], 71), 0),
        "values": gaussian(key_list[2], (PACKED_TOKENS, KEY_VALUE_HEADS * HEAD_WIDTH), 1.0, 6.0, ((0, 128), (1, 2))),
        "out_weight": gaussian(key_list[3], (QUERY_HEADS * HEAD_WIDTH, D), (QUERY_HEADS * HEAD_WIDTH) ** -0.5, 0.125, ((0, 2),)),
        "cotangent": gaussian(key_list[4], (PACKED_TOKENS, D), 1.0, 6.0, ((0, 128), (1, 2))),
        "doc_lengths": uneven(key_list[5], DOCS, PACKED_TOKENS, DOC_MOST, 2).astype(jnp.int32),
    }


def reference(queries, keys, values, out_weight, cotangent, doc_lengths):
    group_width = QUERY_HEADS // KEY_VALUE_HEADS
    score_scale = 1.0 / math.sqrt(HEAD_WIDTH)
    head_window = REACH * SHARD_TOKENS
    span_rows = head_window + SHARD_TOKENS
    block_count = PACKED_TOKENS // SHARD_TOKENS
    doc_ends = jnp.cumsum(doc_lengths).astype(jnp.int32)
    positions = jnp.arange(PACKED_TOKENS, dtype=jnp.int32)
    segments = lax.optimization_barrier(jnp.sum((positions[:, None] >= doc_ends[None, :]).astype(jnp.int32), axis=1)).astype(jnp.int32)
    pad_seg = jnp.concatenate([jnp.full((head_window,), -1, jnp.int32), segments])
    every_query = queries.reshape(PACKED_TOKENS, KEY_VALUE_HEADS, group_width, HEAD_WIDTH)
    padded_keys = jnp.concatenate([jnp.zeros((head_window, KEY_VALUE_HEADS * HEAD_WIDTH), keys.dtype), keys]).reshape(PACKED_TOKENS + head_window, KEY_VALUE_HEADS, HEAD_WIDTH)
    padded_values = jnp.concatenate([jnp.zeros((head_window, KEY_VALUE_HEADS * HEAD_WIDTH), values.dtype), values]).reshape(PACKED_TOKENS + head_window, KEY_VALUE_HEADS, HEAD_WIDTH)
    local_offsets = jnp.arange(SHARD_TOKENS, dtype=jnp.int32)
    span_offsets = jnp.arange(span_rows, dtype=jnp.int32)

    def block_parts(block_id):
        first_row = (block_id * SHARD_TOKENS).astype(jnp.int32)
        query_blk = lax.dynamic_slice_in_dim(every_query, first_row, SHARD_TOKENS, 0).astype(jnp.float32)
        key_blk = lax.dynamic_slice_in_dim(padded_keys, first_row, span_rows, 0).astype(jnp.float32)
        value_blk = lax.dynamic_slice_in_dim(padded_values, first_row, span_rows, 0).astype(jnp.float32)
        query_seg = lax.dynamic_slice_in_dim(segments, first_row, SHARD_TOKENS, 0)
        key_seg = lax.dynamic_slice_in_dim(pad_seg, first_row, span_rows, 0)
        query_pos = first_row + local_offsets
        key_pos = first_row - head_window + span_offsets
        allowed = (query_seg[:, None] == key_seg[None, :]) & (key_pos[None, :] <= query_pos[:, None])
        scores = jnp.einsum('pkgd,jkd->kgpj', query_blk, key_blk) * score_scale
        return (query_blk, key_blk, value_blk, allowed, scores)

    def forward_block(block_id):
        query_blk, key_blk, value_blk, allowed, scores = block_parts(block_id)
        row_max = lax.optimization_barrier(jnp.max(jnp.where(allowed, scores, -jnp.inf), axis=-1, keepdims=True))
        row_mass = lax.optimization_barrier(jnp.sum(jnp.where(allowed, jnp.exp(scores - row_max), 0.0), axis=-1, keepdims=True))
        log_mass = row_max + jnp.log(row_mass)
        prob_low = lax.optimization_barrier(jnp.where(allowed, jnp.exp(scores - log_mass), 0.0).astype(jnp.bfloat16)).astype(jnp.float32)
        output = jnp.einsum('kgpj,jkd->pkgd', prob_low, value_blk)
        return (output.astype(jnp.bfloat16).reshape(SHARD_TOKENS, QUERY_HEADS * HEAD_WIDTH), log_mass)
    block_ids = jnp.arange(block_count, dtype=jnp.int32)
    grouped_attention, log_masses = lax.map(forward_block, block_ids)
    grouped_attention = grouped_attention.reshape(PACKED_TOKENS, QUERY_HEADS * HEAD_WIDTH)
    half_cols = QUERY_HEADS * HEAD_WIDTH // 2
    first_half = jnp.dot(grouped_attention[:, :half_cols], out_weight[:half_cols], preferred_element_type=jnp.float32).astype(jnp.bfloat16)
    second_half = jnp.dot(grouped_attention[:, half_cols:], out_weight[half_cols:], preferred_element_type=jnp.float32).astype(jnp.bfloat16)
    first_half = lax.optimization_barrier(first_half)
    second_half = lax.optimization_barrier(second_half)
    mixed_out = (first_half.astype(jnp.float32) + second_half.astype(jnp.float32)).astype(jnp.bfloat16)
    attention_gradient = lax.dot_general(cotangent, out_weight, (((1,), (1,)), ((), ())), preferred_element_type=jnp.float32).astype(jnp.bfloat16)
    attention_gradient = lax.optimization_barrier(attention_gradient)
    row_delta_terms = lax.optimization_barrier(jnp.sum((attention_gradient.astype(jnp.float32) * grouped_attention.astype(jnp.float32)).reshape(PACKED_TOKENS, KEY_VALUE_HEADS, group_width, HEAD_WIDTH), axis=-1))

    def backward_block(carry, block_id):
        key_gradient_total, value_gradient_total = carry
        query_blk, key_blk, value_blk, allowed, scores = block_parts(block_id)
        first_row = (block_id * SHARD_TOKENS).astype(jnp.int32)
        prob_full = jnp.where(allowed, jnp.exp(scores - log_masses[block_id]), 0.0)
        prob_low = lax.optimization_barrier(prob_full.astype(jnp.bfloat16)).astype(jnp.float32)
        block_gradient = lax.dynamic_slice_in_dim(attention_gradient, first_row, SHARD_TOKENS, 0).reshape(SHARD_TOKENS, KEY_VALUE_HEADS, group_width, HEAD_WIDTH).astype(jnp.float32)
        delta_blk = jnp.transpose(lax.dynamic_slice_in_dim(row_delta_terms, first_row, SHARD_TOKENS, 0), (1, 2, 0))[..., None]
        grad_prob = jnp.einsum('pkgd,jkd->kgpj', block_gradient, value_blk)
        grad_score = lax.optimization_barrier((prob_full * (grad_prob - delta_blk)).astype(jnp.bfloat16)).astype(jnp.float32)
        query_part = jnp.einsum('kgpj,jkd->pkgd', grad_score, key_blk) * score_scale
        key_part = jnp.einsum('kgpj,pkgd->jkd', grad_score, query_blk) * score_scale
        value_part = jnp.einsum('kgpj,pkgd->jkd', prob_low, block_gradient)
        key_gradient_total = lax.dynamic_update_slice_in_dim(key_gradient_total, lax.dynamic_slice_in_dim(key_gradient_total, first_row, span_rows, 0) + key_part, first_row, 0)
        value_gradient_total = lax.dynamic_update_slice_in_dim(value_gradient_total, lax.dynamic_slice_in_dim(value_gradient_total, first_row, span_rows, 0) + value_part, first_row, 0)
        return ((key_gradient_total, value_gradient_total), query_part.astype(jnp.bfloat16).reshape(SHARD_TOKENS, QUERY_HEADS * HEAD_WIDTH))
    initial_totals = (jnp.zeros((PACKED_TOKENS + head_window, KEY_VALUE_HEADS, HEAD_WIDTH), jnp.float32), jnp.zeros((PACKED_TOKENS + head_window, KEY_VALUE_HEADS, HEAD_WIDTH), jnp.float32))
    (key_gradient_total, value_gradient_total), query_grad = lax.scan(backward_block, initial_totals, block_ids)
    query_grad = query_grad.reshape(PACKED_TOKENS, QUERY_HEADS * HEAD_WIDTH)
    keys_gradient = key_gradient_total[head_window:].reshape(PACKED_TOKENS, KEY_VALUE_HEADS * HEAD_WIDTH).astype(jnp.bfloat16)
    values_gradient = value_gradient_total[head_window:].reshape(PACKED_TOKENS, KEY_VALUE_HEADS * HEAD_WIDTH).astype(jnp.bfloat16)
    return (mixed_out, query_grad, keys_gradient, values_gradient)
```

```python
from functools import partial
import math

import jax
import jax.numpy as jnp
from jax import lax
from jax.experimental import pallas as pl
from jax.experimental.pallas import tpu as pltpu
from jax.sharding import PartitionSpec as P

HEAD_WIDTH = 128
HOPS = 4
CHUNKS = 4
NEG = -1e30
MESH = pl.DeviceIdType.MESH
F32 = jnp.float32
BF16 = jnp.bfloat16


def mm(a, b):
    return jnp.dot(a, b, preferred_element_type=F32)


def mm_nt(a, b):
    return lax.dot_general(a, b, (((1,), (1,)), ((), ())), preferred_element_type=F32)


def kernel(
    ctx_size,
    q_hbm, k_hbm, v_hbm, w_hbm, cot_hbm, lens_ref,
    out_hbm, dq_hbm, dk_hbm, dv_hbm,
    q_s, q_t, kv, k_t, v_t, w_v, cot, exps, bias, o_t, o_low, attn,
    row_max, row_sum, stage_max, delta, ga_t, do_t, do_s, dq_t, dkv,
    part_send, part_recv, run_send, run_recv, relay, rs_send, rs_recv, own_out, dq_out, dkv_out,
    load_sem, w_sem, out_sem,
    hop_send, hop_recv, chip_send, chip_recv,
    x_send, x_recv, y_send, y_recv,
    part_ss, part_rs, run_ss, run_rs,
):
    heads, tok, width = q_s.shape
    cols = own_out.shape[2]
    half = CHUNKS * cols
    me = lax.axis_index("ctx")
    tp = lax.axis_index("tp")
    core = lax.rem(me, 2)
    chip = me // 2
    chips = ctx_size // 2
    nxt = lax.rem(chip + 1, chips) * 2 + core
    prv = lax.rem(chip + chips - 1, chips) * 2 + core
    mate = me + 1 - 2 * core
    across = lax.rem(me + ctx_size // 2, ctx_size)
    score_scale = 1.0 / math.sqrt(HEAD_WIDTH)
    log2_scale = score_scale / math.log(2.0)

    def on(ctx_id, tp_id):
        return {"ctx": ctx_id, "tp": tp_id}

    kv_loads = [
        pltpu.make_async_copy(k_hbm, kv.at[0, 0], load_sem.at[0]),
        pltpu.make_async_copy(v_hbm, kv.at[0, 1], load_sem.at[1]),
    ]
    q_loads = [
        pltpu.make_async_copy(q_hbm.at[:, pl.ds(h * width, width)], q_s.at[h], load_sem.at[2 + h])
        for h in range(heads)
    ]
    cot_loads = [
        pltpu.make_async_copy(cot_hbm.at[:, pl.ds(c * cols, cols)], cot.at[0, c], load_sem.at[2 + heads + c])
        for c in range(CHUNKS)
    ]
    w_loads = [
        pltpu.make_async_copy(
            w_hbm.at[:, pl.ds(pl.multiple_of(side * half, half), half)], w_v.at[s], w_sem.at[s]
        )
        for s, side in ((0, tp), (1, 1 - tp))
    ]
    for copy in kv_loads + q_loads:
        copy.start()

    barrier = pltpu.get_barrier_semaphore()
    friends = [(nxt, tp), (prv, tp), (mate, tp), (across, tp), (across, 1 - tp)]
    for friend in friends:
        pl.semaphore_signal(barrier, inc=1, device_id=on(*friend), device_id_type=MESH)
    pl.semaphore_wait(barrier, len(friends))

    def hop(j, i):
        src = (k_hbm if i == 0 else v_hbm) if j == 1 else kv.at[2 * (j - 1), i]
        return pltpu.make_async_remote_copy(
            src_ref=src, dst_ref=kv.at[2 * j, i],
            send_sem=hop_send.at[j - 1, i], recv_sem=hop_recv.at[j - 1, i],
            device_id=on(nxt, tp), device_id_type=MESH,
        )

    def to_mate(j, i):
        turn = j - core
        return pltpu.make_async_remote_copy(
            src_ref=kv.at[2 * j, i], dst_ref=kv.at[2 * turn + 1, i],
            send_sem=chip_send.at[turn, i], recv_sem=chip_recv.at[turn, i],
            device_id=on(mate, tp), device_id_type=MESH,
        )

    def from_mate(j, i):
        return pltpu.make_async_remote_copy(
            src_ref=kv.at[2 * (j - 1), i], dst_ref=kv.at[2 * j - 1, i],
            send_sem=chip_send.at[j - 1, i], recv_sem=chip_recv.at[j - 1, i],
            device_id=on(mate, tp), device_id_type=MESH,
        )

    def forward_hop(j):
        for i in range(2):
            if j > 0:
                hop(j, i).wait_recv()
            if j < HOPS:
                hop(j + 1, i).start()
            if j == 0:
                @pl.when(core == 0)
                def _():
                    kv_loads[i].wait()
                    to_mate(j, i).start()

                @pl.when(core == 1)
                def _():
                    kv_loads[i].wait()
            elif j == HOPS:
                @pl.when(core == 1)
                def _():
                    to_mate(j, i).start()
            else:
                to_mate(j, i).start()

    def x_own(ph, c, src):
        way, i = c // 2, c % 2
        return pltpu.make_async_remote_copy(
            src_ref=src, dst_ref=relay.at[ph, way, i],
            send_sem=x_send.at[ph, way, i], recv_sem=x_recv.at[ph, way, i],
            device_id=on(across, tp if way == 0 else 1 - tp), device_id_type=MESH,
        )

    def x_pass(ph, way, i):
        c = 2 * way + i
        dst = cot.at[1, c] if ph == 0 else rs_recv.at[c]
        return pltpu.make_async_remote_copy(
            src_ref=relay.at[ph, way, i], dst_ref=dst,
            send_sem=y_send.at[ph, way, i], recv_sem=y_recv.at[ph, way, i],
            device_id=on(across, 1 - tp if way == 0 else tp), device_id_type=MESH,
        )

    def own_src(ph, c):
        return cot_hbm.at[:, pl.ds(c * cols, cols)] if ph == 0 else rs_send.at[c]

    def pass_on(ph, i):
        for way in range(2):
            x_own(ph, 2 * way + i, own_src(ph, 2 * way + i)).wait_recv()
            x_pass(ph, way, i).start()

    forward_hop(0)
    for c in (0, 2, 1, 3):
        x_own(0, c, own_src(0, c)).start()
    for copy in cot_loads + w_loads:
        copy.start()

    docs = lens_ref.shape[1]
    lens = jnp.broadcast_to(lens_ref[...].astype(F32), (docs, docs))
    before = lax.broadcasted_iota(jnp.int32, (docs, docs), 1) < lax.broadcasted_iota(
        jnp.int32, (docs, docs), 0
    )
    doc_start = jnp.sum(jnp.where(before, lens, 0.0), axis=1, keepdims=True)
    first = (me * tok).astype(F32)
    pos = lax.broadcasted_iota(jnp.int32, (1, tok), 1).astype(F32) + first
    start = jnp.max(jnp.where(doc_start <= pos, doc_start, 0.0), axis=0, keepdims=True) - first
    key_row = lax.broadcasted_iota(jnp.int32, (tok, tok), 0)
    query_col = lax.broadcasted_iota(jnp.int32, (tok, tok), 1)

    def set_bias(slot, d):
        allowed = key_row.astype(F32) >= start + float(d * tok)
        if d == 0:
            allowed = allowed & (key_row <= query_col)
        bias[slot] = jnp.where(allowed, 0.0, NEG)

    def turn_block(d):
        k_t[d] = kv[d, 0].T
        v_t[d] = kv[d, 1].T

    def fwd_stage(stage, blocks):
        for slot, d in enumerate(blocks):
            turn_block(d)
            set_bias(slot, d)

        def head(h, _):
            scores = [mm(kv[d, 0], q_t[h]) * log2_scale + bias[slot] for slot, d in enumerate(blocks)]
            top = scores[0] if len(scores) == 1 else jnp.maximum(scores[0], scores[1])
            top = jnp.max(top, axis=0, keepdims=True)
            if stage > 0:
                top = jnp.maximum(row_max[h], top)
            mass = None
            acc = None
            for d, s in zip(blocks, scores):
                e = jnp.exp2(s - top)
                exps[d, h] = e
                mass = e if mass is None else mass + e
                term = mm(v_t[d], e.astype(BF16))
                acc = term if acc is None else acc + term
            mass = jnp.sum(mass, axis=0, keepdims=True)
            if stage > 0:
                shrink = jnp.exp2(row_max[h] - top)
                mass = mass + row_sum[h] * shrink
                acc = acc + o_t[h] * shrink
            row_max[h] = top
            row_sum[h] = mass
            stage_max[stage, h] = top
            o_t[h] = acc
            return 0

        lax.fori_loop(0, heads, head, 0, unroll=2)

    def grad_half(s):
        def rows(r, _):
            at = pl.ds(pl.multiple_of(r * 2 * width, 2 * width), 2 * width)
            acc = ga_t[at] if s else None
            for c in range(CHUNKS):
                term = mm_nt(w_v[s, at, c * cols : (c + 1) * cols], cot[s, c])
                acc = term if acc is None else acc + term
            ga_t[at] = acc
            return 0

        lax.fori_loop(0, heads // 2, rows, 0)

    for copy in q_loads:
        copy.wait()
    for h in range(heads):
        q_t[h] = q_s[h].T
    fwd_stage(0, [0])
    for copy in cot_loads:
        copy.wait()
    w_loads[0].wait()
    grad_half(0)
    for j in range(1, HOPS + 1):
        forward_hop(j)
        for i in range(2):
            from_mate(j, i).wait_recv()
        fwd_stage(j, [2 * j - 1, 2 * j])
        if j == 2:
            pass_on(0, 0)
        if j == 4:
            pass_on(0, 1)

    for h in range(heads):
        inverse = 1.0 / row_sum[h]
        low = (o_t[h] * inverse).astype(BF16)
        o_low[h] = low
        attn[:, h * width : (h + 1) * width] = low.T
        for stage in range(HOPS + 1):
            stage_max[stage, h] = jnp.exp2(stage_max[stage, h] - row_max[h]) * inverse
    w_loads[1].wait()
    for c in (0, 2, 1, 3):
        rs_send[c] = mm(attn[...], w_v[1, :, c * cols : (c + 1) * cols]).astype(BF16)
        x_own(1, c, rs_send.at[c]).start()

    for way in range(2):
        for i in range(2):
            x_pass(0, way, i).wait_recv()
    grad_half(1)
    for h in range(heads):
        low = ga_t[h * width : (h + 1) * width].astype(BF16)
        do_t[h] = low
        do_s[h] = low.T
        delta[h] = jnp.sum(low.astype(F32) * o_low[h].astype(F32), axis=0, keepdims=True)

    def bwd_block(stage, d, first_block):
        dkv[...] = jnp.zeros_like(dkv)

        def head(h, _):
            prob = exps[d, h] * stage_max[stage, h]
            grad = prob * (mm(kv[d, 1], do_t[h]) - delta[h])
            prob = prob.astype(BF16)
            grad = grad.astype(BF16)
            dkv[1] += mm(prob, do_s[h])
            dkv[0] += mm(grad, q_s[h])
            term = mm(k_t[d], grad)
            dq_t[h] = term if first_block else dq_t[h] + term
            return 0

        lax.fori_loop(0, heads, head, 0, unroll=2)

    def part(j):
        return pltpu.make_async_remote_copy(
            src_ref=part_send.at[j - 1], dst_ref=part_recv.at[j - 1],
            send_sem=part_ss.at[j - 1], recv_sem=part_rs.at[j - 1],
            device_id=on(mate, tp), device_id_type=MESH,
        )

    def run(j):
        return pltpu.make_async_remote_copy(
            src_ref=run_send.at[j], dst_ref=run_recv.at[j],
            send_sem=run_ss.at[j], recv_sem=run_rs.at[j],
            device_id=on(prv, tp), device_id_type=MESH,
        )

    def add_part(j):
        part(j).wait_recv()
        dkv[...] += part_recv[j - 1].astype(F32)

    for j in range(HOPS, -1, -1):
        if j > 0:
            bwd_block(j, 2 * j - 1, j == HOPS)
            part_send[j - 1] = dkv[...].astype(BF16)
            part(j).start()
        bwd_block(j, 2 * j, False)
        if j < HOPS:
            @pl.when(core == 0)
            def _():
                add_part(j + 1)
        if j > 0:
            @pl.when(core == 1)
            def _():
                add_part(j)
        if j < HOPS:
            run(j).wait_recv()
            dkv[...] += run_recv[j].astype(F32)
        if j > 0:
            run_send[j - 1] = dkv[...].astype(BF16)
            run(j - 1).start()
        if j == 3:
            pass_on(1, 0)
        if j == 1:
            pass_on(1, 1)

    dkv_out[0] = (dkv[0] * score_scale).astype(BF16)
    dkv_out[1] = dkv[1].astype(BF16)
    outs = [
        pltpu.make_async_copy(dkv_out.at[0], dk_hbm, out_sem.at[0]),
        pltpu.make_async_copy(dkv_out.at[1], dv_hbm, out_sem.at[1]),
    ]
    for copy in outs:
        copy.start()
    for h in range(heads):
        dq_out[h] = (dq_t[h] * score_scale).T.astype(BF16)
        copy = pltpu.make_async_copy(dq_out.at[h], dq_hbm.at[:, pl.ds(h * width, width)], out_sem.at[2 + h])
        copy.start()
        outs.append(copy)
    for c in range(CHUNKS):
        own_out[c] = mm(attn[...], w_v[0, :, c * cols : (c + 1) * cols]).astype(BF16)
    for i in range(2):
        for way in range(2):
            c = 2 * way + i
            x_pass(1, way, i).wait_recv()
            own_out[c] = (own_out[c].astype(F32) + rs_recv[c].astype(F32)).astype(BF16)
            copy = pltpu.make_async_copy(
                own_out.at[c], out_hbm.at[:, pl.ds(c * cols, cols)], out_sem.at[2 + heads + c]
            )
            copy.start()
            outs.append(copy)

    for j in range(1, HOPS + 1):
        for i in range(2):
            hop(j, i).wait_send()
            from_mate(j, i).wait_send()
        part(j).wait_send()
        run(j - 1).wait_send()
    for ph in range(2):
        for c in range(CHUNKS):
            x_own(ph, c, own_src(ph, c)).wait_send()
            x_pass(ph, c // 2, c % 2).wait_send()
    for copy in outs:
        copy.wait()


def body(ctx_size, queries, keys, values, out_weight, cotangent, doc_lengths):
    tok = queries.shape[0]
    heads = queries.shape[1] // HEAD_WIDTH
    half = cotangent.shape[1]
    cols = half // CHUNKS
    width = HEAD_WIDTH
    slots = 2 * HOPS + 1
    any_spec = pl.BlockSpec(memory_space=pl.ANY)
    vmem = pltpu.VMEM
    dma = pltpu.SemaphoreType.DMA
    scratch = [
        vmem((heads, tok, width), BF16),
        vmem((heads, width, tok), BF16),
        vmem((slots, 2, tok, width), BF16),
        vmem((slots, width, tok), BF16),
        vmem((slots, width, tok), BF16),
        vmem((2, heads * width, half), BF16),
        vmem((2, CHUNKS, tok, cols), BF16),
        vmem((slots, heads, tok, tok), F32),
        vmem((2, tok, tok), F32),
        vmem((heads, width, tok), F32),
        vmem((heads, width, tok), BF16),
        vmem((tok, heads * width), BF16),
        vmem((heads, 1, tok), F32),
        vmem((heads, 1, tok), F32),
        vmem((HOPS + 1, heads, 1, tok), F32),
        vmem((heads, 1, tok), F32),
        vmem((heads * width, tok), F32),
        vmem((heads, width, tok), BF16),
        vmem((heads, tok, width), BF16),
        vmem((heads, width, tok), F32),
        vmem((2, tok, width), F32),
        vmem((HOPS, 2, tok, width), BF16),
        vmem((HOPS, 2, tok, width), BF16),
        vmem((HOPS, 2, tok, width), BF16),
        vmem((HOPS, 2, tok, width), BF16),
        vmem((2, 2, CHUNKS // 2, tok, cols), BF16),
        vmem((CHUNKS, tok, cols), BF16),
        vmem((CHUNKS, tok, cols), BF16),
        vmem((CHUNKS, tok, cols), BF16),
        vmem((heads, tok, width), BF16),
        vmem((2, tok, width), BF16),
        dma((2 + heads + CHUNKS,)),
        dma((2,)),
        dma((2 + heads + CHUNKS,)),
        dma((HOPS, 2)), dma((HOPS, 2)),
        dma((HOPS, 2)), dma((HOPS, 2)),
        dma((2, 2, CHUNKS // 2)), dma((2, 2, CHUNKS // 2)),
        dma((2, 2, CHUNKS // 2)), dma((2, 2, CHUNKS // 2)),
        dma((HOPS,)), dma((HOPS,)),
        dma((HOPS,)), dma((HOPS,)),
    ]
    return pl.pallas_call(
        partial(kernel, ctx_size),
        out_shape=(
            jax.ShapeDtypeStruct((tok, half), BF16),
            jax.ShapeDtypeStruct((tok, heads * width), BF16),
            jax.ShapeDtypeStruct((tok, width), BF16),
            jax.ShapeDtypeStruct((tok, width), BF16),
        ),
        in_specs=[any_spec] * 5 + [pl.BlockSpec(memory_space=pltpu.VMEM)],
        out_specs=[any_spec] * 4,
        scratch_shapes=scratch,
        compiler_params=pltpu.CompilerParams(
            collective_id=0, has_side_effects=True, vmem_limit_bytes=60 * 1024 * 1024
        ),
    )(queries, keys, values, out_weight, cotangent, doc_lengths.reshape(1, -1))


def solution(mesh):
    in_specs = (P("ctx", "tp"), P("ctx", "tp"), P("ctx", "tp"), P("tp", None), P("ctx", "tp"), P())
    out_specs = (P("ctx", "tp"), P("ctx", "tp"), P("ctx", "tp"), P("ctx", "tp"))
    return jax.shard_map(
        partial(body, mesh.shape["ctx"]), mesh=mesh, in_specs=in_specs, out_specs=out_specs, check_vma=False
    )
```

```python
from functools import partial
import math

import jax
import jax.numpy as jnp
from jax import lax
from jax.experimental import pallas as pl
from jax.experimental.pallas import tpu as pltpu
from jax.sharding import PartitionSpec as P

HEAD_WIDTH = 128
HOPS = 4
CHUNKS = 4
W_PIECES = 4
NEG = -1e30
MESH = pl.DeviceIdType.MESH
F32 = jnp.float32
BF16 = jnp.bfloat16


def mm(a, b):
    return jnp.dot(a, b, preferred_element_type=F32)


def mm_nt(a, b):
    return lax.dot_general(a, b, (((1,), (1,)), ((), ())), preferred_element_type=F32)


def kernel(
    ctx_size,
    q_hbm, k_hbm, v_hbm, w_hbm, cot_hbm, lens_ref,
    own_out, dq_out, dk_out, dv_out,
    q_s, q_t, kv, k_t, v_t, v_pair, w_v, cot, exps, bias, o_t, o_low, attn,
    row_max, row_sum, stage_max, delta, ga_t, do_t, do_s, dq_t, dkv,
    part_send, part_recv, run_send, run_recv, relay, rs_send, rs_recv, prob_low, grad_low,
    load_sem, w_sem,
    hop_send, hop_recv, chip_send, chip_recv,
    x_send, x_recv, y_send, y_recv,
    part_ss, part_rs, run_ss, run_rs,
):
    heads, tok, width = q_s.shape
    half = own_out.shape[1]
    cols = half // CHUNKS
    me = lax.axis_index("ctx")
    tp = lax.axis_index("tp")
    core = lax.rem(me, 2)
    chip = me // 2
    chips = ctx_size // 2
    nxt = lax.rem(chip + 1, chips) * 2 + core
    prv = lax.rem(chip + chips - 1, chips) * 2 + core
    mate = me + 1 - 2 * core
    across = lax.rem(me + ctx_size // 2, ctx_size)
    score_scale = 1.0 / math.sqrt(HEAD_WIDTH)
    log2_scale = score_scale / math.log(2.0)

    def on(ctx_id, tp_id):
        return {"ctx": ctx_id, "tp": tp_id}

    kv_loads = [
        pltpu.make_async_copy(k_hbm, kv.at[0, 0], load_sem.at[0]),
        pltpu.make_async_copy(v_hbm, kv.at[0, 1], load_sem.at[1]),
    ]
    q_loads = [
        pltpu.make_async_copy(q_hbm.at[:, pl.ds(h * width, width)], q_s.at[h], load_sem.at[2 + h])
        for h in range(heads)
    ]
    cot_loads = [
        pltpu.make_async_copy(
            cot_hbm.at[:, pl.ds(c * cols, cols)], cot.at[0, :, pl.ds(c * cols, cols)], load_sem.at[2 + heads + c]
        )
        for c in range(CHUNKS)
    ]
    w_rows = heads * width // W_PIECES
    w_loads = [
        pltpu.make_async_copy(
            w_hbm.at[pl.ds(r * w_rows, w_rows), pl.ds(pl.multiple_of(side * half, half), half)],
            w_v.at[s, pl.ds(r * w_rows, w_rows)],
            w_sem.at[s, r],
        )
        for s, side in ((1, 1 - tp), (0, tp))
        for r in range(W_PIECES)
    ]
    for copy in kv_loads + q_loads:
        copy.start()

    barrier = pltpu.get_barrier_semaphore()
    friends = [(nxt, tp), (prv, tp), (mate, tp), (across, tp), (across, 1 - tp)]
    for friend in friends:
        pl.semaphore_signal(barrier, inc=1, device_id=on(*friend), device_id_type=MESH)
    pl.semaphore_wait(barrier, len(friends))

    def hop(j, i):
        src = (k_hbm, v_hbm)[i] if isinstance(j, int) and j == 1 else kv.at[2 * (j - 1), i]
        return pltpu.make_async_remote_copy(
            src_ref=src, dst_ref=kv.at[2 * j, i],
            send_sem=hop_send.at[j - 1, i], recv_sem=hop_recv.at[j - 1, i],
            device_id=on(nxt, tp), device_id_type=MESH,
        )

    def to_mate(j, i):
        turn = j - core
        return pltpu.make_async_remote_copy(
            src_ref=kv.at[2 * j, i], dst_ref=kv.at[2 * turn + 1, i],
            send_sem=chip_send.at[turn, i], recv_sem=chip_recv.at[turn, i],
            device_id=on(mate, tp), device_id_type=MESH,
        )

    def from_mate(j, i):
        return pltpu.make_async_remote_copy(
            src_ref=kv.at[2 * (j - 1), i], dst_ref=kv.at[2 * j - 1, i],
            send_sem=chip_send.at[j - 1, i], recv_sem=chip_recv.at[j - 1, i],
            device_id=on(mate, tp), device_id_type=MESH,
        )

    def first_hop():
        for i in range(2):
            hop(1, i).start()
            kv_loads[i].wait()

            @pl.when(core == 0)
            def _():
                to_mate(0, i).start()

    def forward_hop(j):
        for i in range(2):
            hop(j, i).wait_recv()

            @pl.when(j < HOPS)
            def _():
                hop(j + 1, i).start()

            @pl.when((j < HOPS) | (core == 1))
            def _():
                to_mate(j, i).start()

    def x_own(ph, c, src):
        way, i = c // 2, c % 2
        return pltpu.make_async_remote_copy(
            src_ref=src, dst_ref=relay.at[ph, way, i],
            send_sem=x_send.at[ph, way, i], recv_sem=x_recv.at[ph, way, i],
            device_id=on(across, tp if way == 0 else 1 - tp), device_id_type=MESH,
        )

    def x_pass(ph, way, i):
        c = 2 * way + i
        dst = cot.at[1, :, pl.ds(c * cols, cols)] if ph == 0 else rs_recv.at[c]
        return pltpu.make_async_remote_copy(
            src_ref=relay.at[ph, way, i], dst_ref=dst,
            send_sem=y_send.at[ph, way, i], recv_sem=y_recv.at[ph, way, i],
            device_id=on(across, 1 - tp if way == 0 else tp), device_id_type=MESH,
        )

    def own_src(ph, c):
        return cot_hbm.at[:, pl.ds(c * cols, cols)] if ph == 0 else rs_send.at[c]

    def pass_on(ph, i):
        for way in range(2):
            x_own(ph, 2 * way + i, own_src(ph, 2 * way + i)).wait_recv()
            x_pass(ph, way, i).start()

    first_hop()
    for c in (0, 2, 1, 3):
        x_own(0, c, own_src(0, c)).start()
    for copy in w_loads + cot_loads:
        copy.start()

    docs = lens_ref.shape[1]
    lens = jnp.broadcast_to(lens_ref[...].astype(F32), (docs, docs))
    before = lax.broadcasted_iota(jnp.int32, (docs, docs), 1) < lax.broadcasted_iota(
        jnp.int32, (docs, docs), 0
    )
    doc_start = jnp.sum(jnp.where(before, lens, 0.0), axis=1, keepdims=True)
    first = (me * tok).astype(F32)
    pos = lax.broadcasted_iota(jnp.int32, (1, tok), 1).astype(F32) + first
    start = jnp.max(jnp.where(doc_start <= pos, doc_start, 0.0), axis=0, keepdims=True) - first
    key_row = lax.broadcasted_iota(jnp.int32, (tok, tok), 0)
    query_col = lax.broadcasted_iota(jnp.int32, (tok, tok), 1)

    def set_bias(slot, d):
        allowed = key_row.astype(F32) >= start + jnp.asarray(d * tok, jnp.int32).astype(F32)
        if isinstance(d, int) and d == 0:
            allowed = allowed & (key_row <= query_col)
        bias[slot] = jnp.where(allowed, 0.0, NEG)

    def fwd_stage(stage, blocks):
        for slot, d in enumerate(blocks):
            k_t[d] = kv[d, 0].T
            turned = kv[d, 1].T
            if len(blocks) == 1:
                v_t[...] = turned
            else:
                v_pair[:, slot * tok : (slot + 1) * tok] = turned
            set_bias(slot, d)

        initial = isinstance(stage, int)
        for h in range(heads):
            scores = [mm(kv[d, 0], q_t[h]) * log2_scale + bias[slot] for slot, d in enumerate(blocks)]
            top = scores[0] if initial else jnp.maximum(scores[0], scores[1])
            top = jnp.max(top, axis=0, keepdims=True)
            if not initial:
                top = jnp.maximum(row_max[h], top)
            mass = None
            low = []
            for d, s in zip(blocks, scores):
                e = jnp.exp2(s - top)
                exps[d, h] = e
                mass = e if mass is None else mass + e
                low.append(e.astype(BF16))
            if initial:
                acc = mm(v_t[...], low[0])
            else:
                acc = mm(v_pair[...], jnp.concatenate(low, axis=0))
            mass = jnp.sum(mass, axis=0, keepdims=True)
            if not initial:
                shrink = jnp.exp2(row_max[h] - top)
                mass = mass + row_sum[h] * shrink
                acc = acc + o_t[h] * shrink
            row_max[h] = top
            row_sum[h] = mass
            stage_max[stage, h] = top
            o_t[h] = acc

    def grad_half(s):
        step = 4 * width
        for r in range(0, heads * width, step):
            term = mm_nt(w_v[s, r : r + step], cot[s])
            ga_t[r : r + step] = ga_t[r : r + step] + term if s else term

    for copy in q_loads:
        copy.wait()
    for h in range(heads):
        q_t[h] = q_s[h].T
    fwd_stage(0, [0])

    def forward_step(j, _):
        forward_hop(j)
        for i in range(2):
            from_mate(j, i).wait_recv()
        fwd_stage(j, [2 * j - 1, 2 * j])

        @pl.when(j == 2)
        def _():
            pass_on(0, 0)

        @pl.when(j == HOPS)
        def _():
            pass_on(0, 1)

        return 0

    lax.fori_loop(1, HOPS + 1, forward_step, 0)

    for h in range(heads):
        inverse = 1.0 / row_sum[h]
        low = (o_t[h] * inverse).astype(BF16)
        o_low[h] = low
        attn[:, h * width : (h + 1) * width] = low.T
        for stage in range(HOPS + 1):
            stage_max[stage, h] = jnp.exp2(stage_max[stage, h] - row_max[h]) * inverse
    for copy in w_loads[:W_PIECES]:
        copy.wait()
    for c in (0, 2, 1, 3):
        rs_send[c] = mm(attn[...], w_v[1, :, c * cols : (c + 1) * cols]).astype(BF16)
        x_own(1, c, rs_send.at[c]).start()

    for copy in w_loads[W_PIECES:] + cot_loads:
        copy.wait()
    grad_half(0)
    for way in range(2):
        for i in range(2):
            x_pass(0, way, i).wait_recv()
    grad_half(1)
    for h in range(heads):
        low = ga_t[h * width : (h + 1) * width].astype(BF16)
        do_t[h] = low
        do_s[h] = low.T
        delta[h] = jnp.sum(low.astype(F32) * o_low[h].astype(F32), axis=0, keepdims=True)

    dq_t[...] = jnp.zeros_like(dq_t)

    def bwd_block(stage, d, slot):
        rows = slice(slot * tok, (slot + 1) * tok)
        for h in range(heads):
            prob = exps[d, h] * stage_max[stage, h]
            grad = prob * (mm(kv[d, 1], do_t[h]) - delta[h])
            prob_low[:, h * tok : (h + 1) * tok] = prob.astype(BF16)
            grad_low[rows, h * tok : (h + 1) * tok] = grad.astype(BF16)
        dkv[1] = mm(prob_low[...], do_s[...].reshape(heads * tok, width))
        dkv[0] = mm(grad_low[rows], q_s[...].reshape(heads * tok, width))

    def add_dq(keys_turned, rows):
        for h in range(heads):
            dq_t[h] += mm(keys_turned, grad_low[:rows, h * tok : (h + 1) * tok])

    def part(j):
        return pltpu.make_async_remote_copy(
            src_ref=part_send.at[j - 1], dst_ref=part_recv.at[j - 1],
            send_sem=part_ss.at[j - 1], recv_sem=part_rs.at[j - 1],
            device_id=on(mate, tp), device_id_type=MESH,
        )

    def run(j):
        return pltpu.make_async_remote_copy(
            src_ref=run_send.at[j], dst_ref=run_recv.at[j],
            send_sem=run_ss.at[j], recv_sem=run_rs.at[j],
            device_id=on(prv, tp), device_id_type=MESH,
        )

    def add_part(j):
        part(j).wait_recv()
        dkv[...] += part_recv[j - 1].astype(F32)

    def run_on(j):
        run(j).wait_recv()
        dkv[...] += run_recv[j].astype(F32)

    def backward_step(it, _):
        j = HOPS - it
        bwd_block(j, 2 * j - 1, 0)
        part_send[j - 1] = dkv[...].astype(BF16)
        part(j).start()
        bwd_block(j, 2 * j, 1)
        add_dq(jnp.concatenate([k_t[2 * j - 1], k_t[2 * j]], axis=1), 2 * tok)

        @pl.when((core == 0) & (j < HOPS))
        def _():
            add_part(j + 1)

        @pl.when(core == 1)
        def _():
            add_part(j)

        @pl.when(j < HOPS)
        def _():
            run_on(j)

        run_send[j - 1] = dkv[...].astype(BF16)
        run(j - 1).start()

        @pl.when(j == 3)
        def _():
            pass_on(1, 0)

        @pl.when(j == 1)
        def _():
            pass_on(1, 1)

        return 0

    lax.fori_loop(0, HOPS, backward_step, 0)
    bwd_block(0, 0, 0)
    add_dq(k_t[0], tok)
    for h in range(heads):
        dq_out[:, h * width : (h + 1) * width] = (dq_t[h] * score_scale).T.astype(BF16)
    for c in range(CHUNKS):
        own_out[:, c * cols : (c + 1) * cols] = mm(attn[...], w_v[0, :, c * cols : (c + 1) * cols]).astype(BF16)

    @pl.when(core == 0)
    def _():
        add_part(1)

    run_on(0)
    dk_out[...] = (dkv[0] * score_scale).astype(BF16)
    dv_out[...] = dkv[1].astype(BF16)
    for i in range(2):
        for way in range(2):
            c = 2 * way + i
            x_pass(1, way, i).wait_recv()
            at = slice(c * cols, (c + 1) * cols)
            own_out[:, at] = (own_out[:, at].astype(F32) + rs_recv[c].astype(F32)).astype(BF16)

    for j in range(1, HOPS + 1):
        for i in range(2):
            hop(j, i).wait_send()
            from_mate(j, i).wait_send()
        part(j).wait_send()
        run(j - 1).wait_send()
    for ph in range(2):
        for c in range(CHUNKS):
            x_own(ph, c, own_src(ph, c)).wait_send()
            x_pass(ph, c // 2, c % 2).wait_send()


def body(ctx_size, queries, keys, values, out_weight, cotangent, doc_lengths):
    tok = queries.shape[0]
    heads = queries.shape[1] // HEAD_WIDTH
    half = cotangent.shape[1]
    cols = half // CHUNKS
    width = HEAD_WIDTH
    slots = 2 * HOPS + 1
    any_spec = pl.BlockSpec(memory_space=pl.ANY)
    vmem = pltpu.VMEM
    dma = pltpu.SemaphoreType.DMA
    scratch = [
        vmem((heads, tok, width), BF16),
        vmem((heads, width, tok), BF16),
        vmem((slots, 2, tok, width), BF16),
        vmem((slots, width, tok), BF16),
        vmem((width, tok), BF16),
        vmem((width, 2 * tok), BF16),
        vmem((2, heads * width, half), BF16),
        vmem((2, tok, half), BF16),
        vmem((slots, heads, tok, tok), F32),
        vmem((2, tok, tok), F32),
        vmem((heads, width, tok), F32),
        vmem((heads, width, tok), BF16),
        vmem((tok, heads * width), BF16),
        vmem((heads, 1, tok), F32),
        vmem((heads, 1, tok), F32),
        vmem((HOPS + 1, heads, 1, tok), F32),
        vmem((heads, 1, tok), F32),
        vmem((heads * width, tok), F32),
        vmem((heads, width, tok), BF16),
        vmem((heads, tok, width), BF16),
        vmem((heads, width, tok), F32),
        vmem((2, tok, width), F32),
        vmem((HOPS, 2, tok, width), BF16),
        vmem((HOPS, 2, tok, width), BF16),
        vmem((HOPS, 2, tok, width), BF16),
        vmem((HOPS, 2, tok, width), BF16),
        vmem((2, 2, CHUNKS // 2, tok, cols), BF16),
        vmem((CHUNKS, tok, cols), BF16),
        vmem((CHUNKS, tok, cols), BF16),
        vmem((tok, heads * tok), BF16),
        vmem((2 * tok, heads * tok), BF16),
        dma((2 + heads + CHUNKS,)),
        dma((2, W_PIECES)),
        dma((HOPS, 2)), dma((HOPS, 2)),
        dma((HOPS, 2)), dma((HOPS, 2)),
        dma((2, 2, CHUNKS // 2)), dma((2, 2, CHUNKS // 2)),
        dma((2, 2, CHUNKS // 2)), dma((2, 2, CHUNKS // 2)),
        dma((HOPS,)), dma((HOPS,)),
        dma((HOPS,)), dma((HOPS,)),
    ]
    shapes = [(tok, half), (tok, heads * width), (tok, width), (tok, width)]
    results = pl.pallas_call(
        partial(kernel, ctx_size),
        out_shape=tuple(pltpu.VMEM(shape, BF16) for shape in shapes),
        in_specs=[any_spec] * 5 + [pl.BlockSpec(memory_space=pltpu.VMEM)],
        out_specs=[pl.BlockSpec(memory_space=pltpu.VMEM)] * 4,
        scratch_shapes=scratch,
        compiler_params=pltpu.CompilerParams(
            collective_id=0, has_side_effects=True, vmem_limit_bytes=60 * 1024 * 1024
        ),
    )(queries, keys, values, out_weight, cotangent, doc_lengths.reshape(1, -1))
    return pl.pallas_call(
        write_out,
        out_shape=tuple(jax.ShapeDtypeStruct(shape, BF16) for shape in shapes),
        in_specs=[pl.BlockSpec(memory_space=pltpu.VMEM)] * 4,
        out_specs=[any_spec] * 4,
        scratch_shapes=[dma((4,))],
    )(*[pltpu.with_memory_space_constraint(result, pltpu.VMEM) for result in results])


def write_out(*refs):
    sources, targets, sem = refs[:4], refs[4:8], refs[8]
    copies = [pltpu.make_async_copy(a, b, sem.at[i]) for i, (a, b) in enumerate(zip(sources, targets))]
    for copy in copies:
        copy.start()
    for copy in copies:
        copy.wait()


def solution(mesh):
    in_specs = (P("ctx", "tp"), P("ctx", "tp"), P("ctx", "tp"), P("tp", None), P("ctx", "tp"), P())
    out_specs = (P("ctx", "tp"), P("ctx", "tp"), P("ctx", "tp"), P("ctx", "tp"))
    return jax.shard_map(
        partial(body, mesh.shape["ctx"]), mesh=mesh, in_specs=in_specs, out_specs=out_specs, check_vma=False
    )
```

```python
from functools import partial
import math

import jax
import jax.numpy as jnp
from jax import lax
from jax.experimental import pallas as pl
from jax.experimental.pallas import tpu as pltpu
from jax.sharding import PartitionSpec as P

HEAD_WIDTH = 128
HOPS = 4
CHUNKS = 4
W_PIECES = 4
PIECE = 128
NEG = -1e30
MESH = pl.DeviceIdType.MESH
F32 = jnp.float32
BF16 = jnp.bfloat16


def mm(a, b):
    return jnp.dot(a, b, preferred_element_type=F32)


def mm_nt(a, b):
    return lax.dot_general(a, b, (((1,), (1,)), ((), ())), preferred_element_type=F32)


def kernel(
    ctx_size,
    q_hbm, k_hbm, v_hbm, w_hbm, cot_hbm, lens_ref,
    own_out, dq_out, dk_out, dv_out,
    q_s, q_t, kv, k_t, v_t, v_pair, w_v, cot, exps, bias, o_t, o_low, attn,
    row_max, row_sum, stage_max, delta, ga_t, do_t, do_s, dq_t, dkv,
    part_send, part_recv, run_send, run_recv, relay, rs_send, rs_recv, prob_low, grad_low,
    score_buf, exp_low,
    load_sem, w_sem,
    hop_send, hop_recv, chip_send, chip_recv,
    x_send, x_recv, y_send, y_recv,
    part_ss, part_rs, run_ss, run_rs,
):
    heads, tok, width = q_s.shape
    half = own_out.shape[1]
    cols = half // CHUNKS
    me = lax.axis_index("ctx")
    tp = lax.axis_index("tp")
    core = lax.rem(me, 2)
    chip = me // 2
    chips = ctx_size // 2
    nxt = lax.rem(chip + 1, chips) * 2 + core
    prv = lax.rem(chip + chips - 1, chips) * 2 + core
    mate = me + 1 - 2 * core
    across = lax.rem(me + ctx_size // 2, ctx_size)
    score_scale = 1.0 / math.sqrt(HEAD_WIDTH)
    log2_scale = score_scale / math.log(2.0)

    def on(ctx_id, tp_id):
        return {"ctx": ctx_id, "tp": tp_id}

    kv_loads = [
        pltpu.make_async_copy(k_hbm, kv.at[0, 0], load_sem.at[0]),
        pltpu.make_async_copy(v_hbm, kv.at[0, 1], load_sem.at[1]),
    ]
    q_loads = [
        pltpu.make_async_copy(q_hbm.at[:, pl.ds(h * width, width)], q_s.at[h], load_sem.at[2 + h])
        for h in range(heads)
    ]
    cot_loads = [
        pltpu.make_async_copy(
            cot_hbm.at[:, pl.ds(c * cols, cols)], cot.at[0, :, pl.ds(c * cols, cols)], load_sem.at[2 + heads + c]
        )
        for c in range(CHUNKS)
    ]
    w_rows = heads * width // W_PIECES
    w_loads = [
        pltpu.make_async_copy(
            w_hbm.at[pl.ds(r * w_rows, w_rows), pl.ds(pl.multiple_of(side * half, half), half)],
            w_v.at[s, pl.ds(r * w_rows, w_rows)],
            w_sem.at[s, r],
        )
        for s, side in ((1, 1 - tp), (0, tp))
        for r in range(W_PIECES)
    ]
    for copy in kv_loads + q_loads:
        copy.start()

    barrier = pltpu.get_barrier_semaphore()
    friends = [(nxt, tp), (prv, tp), (mate, tp), (across, tp), (across, 1 - tp)]
    for friend in friends:
        pl.semaphore_signal(barrier, inc=1, device_id=on(*friend), device_id_type=MESH)
    pl.semaphore_wait(barrier, len(friends))

    def hop(j, i):
        src = (k_hbm, v_hbm)[i] if isinstance(j, int) and j == 1 else kv.at[2 * (j - 1), i]
        return pltpu.make_async_remote_copy(
            src_ref=src, dst_ref=kv.at[2 * j, i],
            send_sem=hop_send.at[j - 1, i], recv_sem=hop_recv.at[j - 1, i],
            device_id=on(nxt, tp), device_id_type=MESH,
        )

    def to_mate(j, i):
        turn = j - core
        return pltpu.make_async_remote_copy(
            src_ref=kv.at[2 * j, i], dst_ref=kv.at[2 * turn + 1, i],
            send_sem=chip_send.at[turn, i], recv_sem=chip_recv.at[turn, i],
            device_id=on(mate, tp), device_id_type=MESH,
        )

    def from_mate(j, i):
        return pltpu.make_async_remote_copy(
            src_ref=kv.at[2 * (j - 1), i], dst_ref=kv.at[2 * j - 1, i],
            send_sem=chip_send.at[j - 1, i], recv_sem=chip_recv.at[j - 1, i],
            device_id=on(mate, tp), device_id_type=MESH,
        )

    def first_hop():
        for i in range(2):
            hop(1, i).start()
            kv_loads[i].wait()

            @pl.when(core == 0)
            def _():
                to_mate(0, i).start()

    def forward_hop(j):
        for i in range(2):
            hop(j, i).wait_recv()

            @pl.when(j < HOPS)
            def _():
                hop(j + 1, i).start()

            @pl.when((j < HOPS) | (core == 1))
            def _():
                to_mate(j, i).start()

    def x_own(ph, c, src):
        way, i = c // 2, c % 2
        return pltpu.make_async_remote_copy(
            src_ref=src, dst_ref=relay.at[ph, way, i],
            send_sem=x_send.at[ph, way, i], recv_sem=x_recv.at[ph, way, i],
            device_id=on(across, tp if way == 0 else 1 - tp), device_id_type=MESH,
        )

    def x_pass(ph, way, i):
        c = 2 * way + i
        dst = cot.at[1, :, pl.ds(c * cols, cols)] if ph == 0 else rs_recv.at[c]
        return pltpu.make_async_remote_copy(
            src_ref=relay.at[ph, way, i], dst_ref=dst,
            send_sem=y_send.at[ph, way, i], recv_sem=y_recv.at[ph, way, i],
            device_id=on(across, 1 - tp if way == 0 else tp), device_id_type=MESH,
        )

    def own_src(ph, c):
        return cot_hbm.at[:, pl.ds(c * cols, cols)] if ph == 0 else rs_send.at[c]

    def pass_on(ph, i):
        for way in range(2):
            x_own(ph, 2 * way + i, own_src(ph, 2 * way + i)).wait_recv()
            x_pass(ph, way, i).start()

    first_hop()
    for c in (0, 2, 1, 3):
        x_own(0, c, own_src(0, c)).start()
    for copy in w_loads + cot_loads:
        copy.start()

    docs = lens_ref.shape[1]
    lens = jnp.broadcast_to(lens_ref[...].astype(F32), (docs, docs))
    before = lax.broadcasted_iota(jnp.int32, (docs, docs), 1) < lax.broadcasted_iota(
        jnp.int32, (docs, docs), 0
    )
    doc_start = jnp.sum(jnp.where(before, lens, 0.0), axis=1, keepdims=True)
    first = (me * tok).astype(F32)
    pos = lax.broadcasted_iota(jnp.int32, (1, tok), 1).astype(F32) + first
    start = jnp.max(jnp.where(doc_start <= pos, doc_start, 0.0), axis=0, keepdims=True) - first
    key_row = lax.broadcasted_iota(jnp.int32, (tok, tok), 0)
    query_col = lax.broadcasted_iota(jnp.int32, (tok, tok), 1)

    def set_bias(slot, d):
        allowed = key_row.astype(F32) >= start + jnp.asarray(d * tok, jnp.int32).astype(F32)
        if isinstance(d, int) and d == 0:
            allowed = allowed & (key_row <= query_col)
        bias[slot] = jnp.where(allowed, 0.0, NEG)

    def fwd_stage(stage, blocks):
        for slot, d in enumerate(blocks):
            k_t[d] = kv[d, 0].T
            turned = kv[d, 1].T
            if len(blocks) == 1:
                v_t[...] = turned
            else:
                v_pair[:, slot * tok : (slot + 1) * tok] = turned
            set_bias(slot, d)

        initial = isinstance(stage, int)
        pieces = [(slot, d, r) for slot, d in enumerate(blocks) for r in range(0, tok, PIECE)]

        def score_piece(h, piece, top):
            slot, d, r = piece
            s = mm(kv[d, 0, r : r + PIECE], q_t[h]) * log2_scale + bias[slot, r : r + PIECE]
            score_buf[h % 2, slot, r : r + PIECE] = s
            part_top = jnp.max(s.reshape(PIECE // 8, 8, tok), axis=0)
            return part_top if top is None else jnp.maximum(top, part_top)

        def exp_piece(h, piece, top, mass):
            slot, d, r = piece
            e = jnp.exp2(score_buf[h % 2, slot, r : r + PIECE] - top)
            exps[d, h, r : r + PIECE] = e
            exp_low[h % 2, slot * tok + r : slot * tok + r + PIECE] = e.astype(BF16)
            part_mass = jnp.sum(e.reshape(PIECE // 8, 8, tok), axis=0)
            return part_mass if mass is None else mass + part_mass

        coming = None
        for piece in pieces:
            coming = score_piece(0, piece, coming)
        for h in range(heads):
            top = jnp.max(coming, axis=0, keepdims=True)
            if not initial:
                top = jnp.maximum(row_max[h], top)
            coming, mass = None, None
            for piece in pieces:
                if h + 1 < heads:
                    coming = score_piece(h + 1, piece, coming)
                mass = exp_piece(h, piece, top, mass)
            if initial:
                acc = mm(v_t[...], exp_low[h % 2, :tok])
            else:
                acc = mm(v_pair[...], exp_low[h % 2])
            mass = jnp.sum(mass, axis=0, keepdims=True)
            if not initial:
                shrink = jnp.exp2(row_max[h] - top)
                mass = mass + row_sum[h] * shrink
                acc = acc + o_t[h] * shrink
            row_max[h] = top
            row_sum[h] = mass
            stage_max[stage, h] = top
            o_t[h] = acc

    def grad_half(s):
        step = 4 * width
        for r in range(0, heads * width, step):
            term = mm_nt(w_v[s, r : r + step], cot[s])
            ga_t[r : r + step] = ga_t[r : r + step] + term if s else term

    for copy in q_loads:
        copy.wait()
    for h in range(heads):
        q_t[h] = q_s[h].T
    fwd_stage(0, [0])

    def forward_step(j, _):
        forward_hop(j)
        for i in range(2):
            from_mate(j, i).wait_recv()
        fwd_stage(j, [2 * j - 1, 2 * j])

        @pl.when(j == 2)
        def _():
            pass_on(0, 0)

        @pl.when(j == HOPS)
        def _():
            pass_on(0, 1)

        return 0

    lax.fori_loop(1, HOPS + 1, forward_step, 0)

    for h in range(heads):
        inverse = 1.0 / row_sum[h]
        low = (o_t[h] * inverse).astype(BF16)
        o_low[h] = low
        attn[:, h * width : (h + 1) * width] = low.T
        for stage in range(HOPS + 1):
            stage_max[stage, h] = jnp.exp2(stage_max[stage, h] - row_max[h]) * inverse
    for copy in w_loads[:W_PIECES]:
        copy.wait()
    for c in (0, 2, 1, 3):
        rs_send[c] = mm(attn[...], w_v[1, :, c * cols : (c + 1) * cols]).astype(BF16)
        x_own(1, c, rs_send.at[c]).start()

    for copy in w_loads[W_PIECES:] + cot_loads:
        copy.wait()
    grad_half(0)
    for way in range(2):
        for i in range(2):
            x_pass(0, way, i).wait_recv()
    grad_half(1)
    for h in range(heads):
        low = ga_t[h * width : (h + 1) * width].astype(BF16)
        do_t[h] = low
        do_s[h] = low.T
        delta[h] = jnp.sum(low.astype(F32) * o_low[h].astype(F32), axis=0, keepdims=True)

    dq_t[...] = jnp.zeros_like(dq_t)

    def bwd_block(stage, d, slot):
        rows = slice(slot * tok, (slot + 1) * tok)
        for h in range(heads):
            prob = exps[d, h] * stage_max[stage, h]
            grad = prob * (mm(kv[d, 1], do_t[h]) - delta[h])
            prob_low[:, h * tok : (h + 1) * tok] = prob.astype(BF16)
            grad_low[rows, h * tok : (h + 1) * tok] = grad.astype(BF16)
        dkv[1] = mm(prob_low[...], do_s[...].reshape(heads * tok, width))
        dkv[0] = mm(grad_low[rows], q_s[...].reshape(heads * tok, width))

    def add_dq(keys_turned, rows):
        for h in range(heads):
            dq_t[h] += mm(keys_turned, grad_low[:rows, h * tok : (h + 1) * tok])

    def part(j):
        return pltpu.make_async_remote_copy(
            src_ref=part_send.at[j - 1], dst_ref=part_recv.at[j - 1],
            send_sem=part_ss.at[j - 1], recv_sem=part_rs.at[j - 1],
            device_id=on(mate, tp), device_id_type=MESH,
        )

    def run(j):
        return pltpu.make_async_remote_copy(
            src_ref=run_send.at[j], dst_ref=run_recv.at[j],
            send_sem=run_ss.at[j], recv_sem=run_rs.at[j],
            device_id=on(prv, tp), device_id_type=MESH,
        )

    def add_part(j):
        part(j).wait_recv()
        dkv[...] += part_recv[j - 1].astype(F32)

    def run_on(j):
        run(j).wait_recv()
        dkv[...] += run_recv[j].astype(F32)

    def backward_step(it, _):
        j = HOPS - it
        bwd_block(j, 2 * j - 1, 0)
        part_send[j - 1] = dkv[...].astype(BF16)
        part(j).start()
        bwd_block(j, 2 * j, 1)
        add_dq(jnp.concatenate([k_t[2 * j - 1], k_t[2 * j]], axis=1), 2 * tok)

        @pl.when((core == 0) & (j < HOPS))
        def _():
            add_part(j + 1)

        @pl.when(core == 1)
        def _():
            add_part(j)

        @pl.when(j < HOPS)
        def _():
            run_on(j)

        run_send[j - 1] = dkv[...].astype(BF16)
        run(j - 1).start()

        @pl.when(j == 3)
        def _():
            pass_on(1, 0)

        @pl.when(j == 1)
        def _():
            pass_on(1, 1)

        return 0

    lax.fori_loop(0, HOPS, backward_step, 0)
    bwd_block(0, 0, 0)
    add_dq(k_t[0], tok)
    for h in range(heads):
        dq_out[:, h * width : (h + 1) * width] = (dq_t[h] * score_scale).T.astype(BF16)
    for c in range(CHUNKS):
        own_out[:, c * cols : (c + 1) * cols] = mm(attn[...], w_v[0, :, c * cols : (c + 1) * cols]).astype(BF16)

    @pl.when(core == 0)
    def _():
        add_part(1)

    run_on(0)
    dk_out[...] = (dkv[0] * score_scale).astype(BF16)
    dv_out[...] = dkv[1].astype(BF16)
    for i in range(2):
        for way in range(2):
            c = 2 * way + i
            x_pass(1, way, i).wait_recv()
            at = slice(c * cols, (c + 1) * cols)
            own_out[:, at] = (own_out[:, at].astype(F32) + rs_recv[c].astype(F32)).astype(BF16)

    for j in range(1, HOPS + 1):
        for i in range(2):
            hop(j, i).wait_send()
            from_mate(j, i).wait_send()
        part(j).wait_send()
        run(j - 1).wait_send()
    for ph in range(2):
        for c in range(CHUNKS):
            x_own(ph, c, own_src(ph, c)).wait_send()
            x_pass(ph, c // 2, c % 2).wait_send()


def body(ctx_size, queries, keys, values, out_weight, cotangent, doc_lengths):
    tok = queries.shape[0]
    heads = queries.shape[1] // HEAD_WIDTH
    half = cotangent.shape[1]
    cols = half // CHUNKS
    width = HEAD_WIDTH
    slots = 2 * HOPS + 1
    any_spec = pl.BlockSpec(memory_space=pl.ANY)
    vmem = pltpu.VMEM
    dma = pltpu.SemaphoreType.DMA
    scratch = [
        vmem((heads, tok, width), BF16),
        vmem((heads, width, tok), BF16),
        vmem((slots, 2, tok, width), BF16),
        vmem((slots, width, tok), BF16),
        vmem((width, tok), BF16),
        vmem((width, 2 * tok), BF16),
        vmem((2, heads * width, half), BF16),
        vmem((2, tok, half), BF16),
        vmem((slots, heads, tok, tok), F32),
        vmem((2, tok, tok), F32),
        vmem((heads, width, tok), F32),
        vmem((heads, width, tok), BF16),
        vmem((tok, heads * width), BF16),
        vmem((heads, 1, tok), F32),
        vmem((heads, 1, tok), F32),
        vmem((HOPS + 1, heads, 1, tok), F32),
        vmem((heads, 1, tok), F32),
        vmem((heads * width, tok), F32),
        vmem((heads, width, tok), BF16),
        vmem((heads, tok, width), BF16),
        vmem((heads, width, tok), F32),
        vmem((2, tok, width), F32),
        vmem((HOPS, 2, tok, width), BF16),
        vmem((HOPS, 2, tok, width), BF16),
        vmem((HOPS, 2, tok, width), BF16),
        vmem((HOPS, 2, tok, width), BF16),
        vmem((2, 2, CHUNKS // 2, tok, cols), BF16),
        vmem((CHUNKS, tok, cols), BF16),
        vmem((CHUNKS, tok, cols), BF16),
        vmem((tok, heads * tok), BF16),
        vmem((2 * tok, heads * tok), BF16),
        vmem((2, 2, tok, tok), F32),
        vmem((2, 2 * tok, tok), BF16),
        dma((2 + heads + CHUNKS,)),
        dma((2, W_PIECES)),
        dma((HOPS, 2)), dma((HOPS, 2)),
        dma((HOPS, 2)), dma((HOPS, 2)),
        dma((2, 2, CHUNKS // 2)), dma((2, 2, CHUNKS // 2)),
        dma((2, 2, CHUNKS // 2)), dma((2, 2, CHUNKS // 2)),
        dma((HOPS,)), dma((HOPS,)),
        dma((HOPS,)), dma((HOPS,)),
    ]
    shapes = [(tok, half), (tok, heads * width), (tok, width), (tok, width)]
    results = pl.pallas_call(
        partial(kernel, ctx_size),
        out_shape=tuple(pltpu.VMEM(shape, BF16) for shape in shapes),
        in_specs=[any_spec] * 5 + [pl.BlockSpec(memory_space=pltpu.VMEM)],
        out_specs=[pl.BlockSpec(memory_space=pltpu.VMEM)] * 4,
        scratch_shapes=scratch,
        compiler_params=pltpu.CompilerParams(
            collective_id=0, has_side_effects=True, vmem_limit_bytes=60 * 1024 * 1024
        ),
    )(queries, keys, values, out_weight, cotangent, doc_lengths.reshape(1, -1))
    return pl.pallas_call(
        write_out,
        out_shape=tuple(jax.ShapeDtypeStruct(shape, BF16) for shape in shapes),
        in_specs=[pl.BlockSpec(memory_space=pltpu.VMEM)] * 4,
        out_specs=[any_spec] * 4,
        scratch_shapes=[dma((4,))],
    )(*[pltpu.with_memory_space_constraint(result, pltpu.VMEM) for result in results])


def write_out(*refs):
    sources, targets, sem = refs[:4], refs[4:8], refs[8]
    copies = [pltpu.make_async_copy(a, b, sem.at[i]) for i, (a, b) in enumerate(zip(sources, targets))]
    for copy in copies:
        copy.start()
    for copy in copies:
        copy.wait()


def solution(mesh):
    in_specs = (P("ctx", "tp"), P("ctx", "tp"), P("ctx", "tp"), P("tp", None), P("ctx", "tp"), P())
    out_specs = (P("ctx", "tp"), P("ctx", "tp"), P("ctx", "tp"), P("ctx", "tp"))
    return jax.shard_map(
        partial(body, mesh.shape["ctx"]), mesh=mesh, in_specs=in_specs, out_specs=out_specs, check_vma=False
    )
```

```python
from functools import partial
import math

import jax
import jax.numpy as jnp
from jax import lax
from jax.experimental import pallas as pl
from jax.experimental.pallas import tpu as pltpu
from jax.sharding import PartitionSpec as P

HEAD_WIDTH = 128
HOPS = 4
CHUNKS = 4
W_PIECES = 4
PIECE = 128
NEG = -1e30
MESH = pl.DeviceIdType.MESH
F32 = jnp.float32
BF16 = jnp.bfloat16


def mm(a, b):
    return jnp.dot(a, b, preferred_element_type=F32)


def mm_nt(a, b):
    return lax.dot_general(a, b, (((1,), (1,)), ((), ())), preferred_element_type=F32)


def kernel(
    ctx_size,
    q_hbm, k_hbm, v_hbm, w_hbm, cot_hbm, lens_ref,
    own_out, dq_out, dk_out, dv_out,
    q_s, q_t, kv, k_t, v_t, v_pair, w_v, cot, exps, bias, o_t, o_low, attn,
    row_max, row_sum, stage_max, delta, ga_t, do_t, do_s, dq_t, dkv,
    part_send, part_recv, run_send, run_recv, relay, rs_send, rs_recv, prob_low, grad_low,
    score_buf, exp_low,
    load_sem, w_sem,
    hop_send, hop_recv, chip_send, chip_recv,
    x_send, x_recv, y_send, y_recv,
    part_ss, part_rs, run_ss, run_rs,
):
    heads, tok, width = q_s.shape
    half = own_out.shape[1]
    cols = half // CHUNKS
    me = lax.axis_index("ctx")
    tp = lax.axis_index("tp")
    core = lax.rem(me, 2)
    chip = me // 2
    chips = ctx_size // 2
    nxt = lax.rem(chip + 1, chips) * 2 + core
    prv = lax.rem(chip + chips - 1, chips) * 2 + core
    mate = me + 1 - 2 * core
    across = lax.rem(me + ctx_size // 2, ctx_size)
    score_scale = 1.0 / math.sqrt(HEAD_WIDTH)
    log2_scale = score_scale / math.log(2.0)

    def on(ctx_id, tp_id):
        return {"ctx": ctx_id, "tp": tp_id}

    kv_loads = [
        pltpu.make_async_copy(k_hbm, kv.at[0, 0], load_sem.at[0]),
        pltpu.make_async_copy(v_hbm, kv.at[0, 1], load_sem.at[1]),
    ]
    q_loads = [
        pltpu.make_async_copy(q_hbm.at[:, pl.ds(h * width, width)], q_s.at[h], load_sem.at[2 + h])
        for h in range(heads)
    ]
    cot_loads = [
        pltpu.make_async_copy(
            cot_hbm.at[:, pl.ds(c * cols, cols)], cot.at[0, :, pl.ds(c * cols, cols)], load_sem.at[2 + heads + c]
        )
        for c in range(CHUNKS)
    ]
    w_rows = heads * width // W_PIECES
    w_loads = [
        pltpu.make_async_copy(
            w_hbm.at[pl.ds(r * w_rows, w_rows), pl.ds(pl.multiple_of(side * half, half), half)],
            w_v.at[s, pl.ds(r * w_rows, w_rows)],
            w_sem.at[s, r],
        )
        for s, side in ((1, 1 - tp), (0, tp))
        for r in range(W_PIECES)
    ]
    for copy in kv_loads + q_loads:
        copy.start()

    barrier = pltpu.get_barrier_semaphore()
    friends = [(nxt, tp), (prv, tp), (mate, tp), (across, tp), (across, 1 - tp)]
    for friend in friends:
        pl.semaphore_signal(barrier, inc=1, device_id=on(*friend), device_id_type=MESH)
    pl.semaphore_wait(barrier, len(friends))

    def hop(j, i):
        src = (k_hbm, v_hbm)[i] if isinstance(j, int) and j == 1 else kv.at[2 * (j - 1), i]
        return pltpu.make_async_remote_copy(
            src_ref=src, dst_ref=kv.at[2 * j, i],
            send_sem=hop_send.at[j - 1, i], recv_sem=hop_recv.at[j - 1, i],
            device_id=on(nxt, tp), device_id_type=MESH,
        )

    def to_mate(j, i):
        turn = j - core
        return pltpu.make_async_remote_copy(
            src_ref=kv.at[2 * j, i], dst_ref=kv.at[2 * turn + 1, i],
            send_sem=chip_send.at[turn, i], recv_sem=chip_recv.at[turn, i],
            device_id=on(mate, tp), device_id_type=MESH,
        )

    def from_mate(j, i):
        return pltpu.make_async_remote_copy(
            src_ref=kv.at[2 * (j - 1), i], dst_ref=kv.at[2 * j - 1, i],
            send_sem=chip_send.at[j - 1, i], recv_sem=chip_recv.at[j - 1, i],
            device_id=on(mate, tp), device_id_type=MESH,
        )

    def first_hop():
        for i in range(2):
            hop(1, i).start()
            kv_loads[i].wait()

            @pl.when(core == 0)
            def _():
                to_mate(0, i).start()

    def forward_hop(j):
        for i in range(2):
            hop(j, i).wait_recv()

            @pl.when(j < HOPS)
            def _():
                hop(j + 1, i).start()

            @pl.when((j < HOPS) | (core == 1))
            def _():
                to_mate(j, i).start()

    def x_own(ph, c, src):
        way, i = c // 2, c % 2
        return pltpu.make_async_remote_copy(
            src_ref=src, dst_ref=relay.at[ph, way, i],
            send_sem=x_send.at[ph, way, i], recv_sem=x_recv.at[ph, way, i],
            device_id=on(across, tp if way == 0 else 1 - tp), device_id_type=MESH,
        )

    def x_pass(ph, way, i):
        c = 2 * way + i
        dst = cot.at[1, :, pl.ds(c * cols, cols)] if ph == 0 else rs_recv.at[c]
        return pltpu.make_async_remote_copy(
            src_ref=relay.at[ph, way, i], dst_ref=dst,
            send_sem=y_send.at[ph, way, i], recv_sem=y_recv.at[ph, way, i],
            device_id=on(across, 1 - tp if way == 0 else tp), device_id_type=MESH,
        )

    def own_src(ph, c):
        return cot_hbm.at[:, pl.ds(c * cols, cols)] if ph == 0 else rs_send.at[c]

    def pass_on(ph, i):
        for way in range(2):
            x_own(ph, 2 * way + i, own_src(ph, 2 * way + i)).wait_recv()
            x_pass(ph, way, i).start()

    first_hop()
    for c in (0, 2, 1, 3):
        x_own(0, c, own_src(0, c)).start()
    for copy in w_loads + cot_loads:
        copy.start()

    docs = lens_ref.shape[1]
    lens = jnp.broadcast_to(lens_ref[...].astype(F32), (docs, docs))
    before = lax.broadcasted_iota(jnp.int32, (docs, docs), 1) < lax.broadcasted_iota(
        jnp.int32, (docs, docs), 0
    )
    doc_start = jnp.sum(jnp.where(before, lens, 0.0), axis=1, keepdims=True)
    first = (me * tok).astype(F32)
    pos = lax.broadcasted_iota(jnp.int32, (1, tok), 1).astype(F32) + first
    start = jnp.max(jnp.where(doc_start <= pos, doc_start, 0.0), axis=0, keepdims=True) - first
    key_row = lax.broadcasted_iota(jnp.int32, (tok, tok), 0)
    query_col = lax.broadcasted_iota(jnp.int32, (tok, tok), 1)

    def set_bias(slot, d):
        allowed = key_row.astype(F32) >= start + jnp.asarray(d * tok, jnp.int32).astype(F32)
        if isinstance(d, int) and d == 0:
            allowed = allowed & (key_row <= query_col)
        bias[slot] = jnp.where(allowed, 0.0, NEG)

    def fwd_stage(stage, blocks):
        for slot, d in enumerate(blocks):
            k_t[d] = kv[d, 0].T
            turned = kv[d, 1].T
            if len(blocks) == 1:
                v_t[...] = turned
            else:
                v_pair[:, slot * tok : (slot + 1) * tok] = turned
            set_bias(slot, d)

        initial = isinstance(stage, int)
        pieces = [(slot, d, r) for slot, d in enumerate(blocks) for r in range(0, tok, PIECE)]

        def score_piece(h, piece, top):
            slot, d, r = piece
            s = mm(kv[d, 0, r : r + PIECE], q_t[h]) * log2_scale + bias[slot, r : r + PIECE]
            score_buf[h % 2, slot, r : r + PIECE] = s
            part_top = jnp.max(s.reshape(PIECE // 8, 8, tok), axis=0)
            return part_top if top is None else jnp.maximum(top, part_top)

        def exp_piece(h, piece, top, mass):
            slot, d, r = piece
            e = jnp.exp2(score_buf[h % 2, slot, r : r + PIECE] - top)
            exps[d, h, r : r + PIECE] = e
            exp_low[h % 2, slot * tok + r : slot * tok + r + PIECE] = e.astype(BF16)
            part_mass = jnp.sum(e.reshape(PIECE // 8, 8, tok), axis=0)
            return part_mass if mass is None else mass + part_mass

        coming = None
        for piece in pieces:
            coming = score_piece(0, piece, coming)
        for h in range(heads):
            top = jnp.max(coming, axis=0, keepdims=True)
            if not initial:
                top = jnp.maximum(row_max[h], top)
            coming, mass = None, None
            for piece in pieces:
                if h + 1 < heads:
                    coming = score_piece(h + 1, piece, coming)
                mass = exp_piece(h, piece, top, mass)
            if initial:
                acc = mm(v_t[...], exp_low[h % 2, :tok])
            else:
                acc = mm(v_pair[...], exp_low[h % 2])
            mass = jnp.sum(mass, axis=0, keepdims=True)
            if not initial:
                shrink = jnp.exp2(row_max[h] - top)
                mass = mass + row_sum[h] * shrink
                acc = acc + o_t[h] * shrink
            row_max[h] = top
            row_sum[h] = mass
            stage_max[stage, h] = top
            o_t[h] = acc

    def grad_half(s):
        step = 4 * width
        for r in range(0, heads * width, step):
            term = mm_nt(w_v[s, r : r + step], cot[s])
            ga_t[r : r + step] = ga_t[r : r + step] + term if s else term

    for copy in q_loads:
        copy.wait()
    for h in range(heads):
        q_t[h] = q_s[h].T
    fwd_stage(0, [0])

    def forward_step(j, _):
        forward_hop(j)
        for i in range(2):
            from_mate(j, i).wait_recv()

        @pl.when(j == 2)
        def _():
            pass_on(0, 0)

        @pl.when(j == HOPS)
        def _():
            pass_on(0, 1)

        fwd_stage(j, [2 * j - 1, 2 * j])
        return 0

    lax.fori_loop(1, HOPS + 1, forward_step, 0)

    for h in range(heads):
        inverse = 1.0 / row_sum[h]
        low = (o_t[h] * inverse).astype(BF16)
        o_low[h] = low
        attn[:, h * width : (h + 1) * width] = low.T
        for stage in range(HOPS + 1):
            stage_max[stage, h] = jnp.exp2(stage_max[stage, h] - row_max[h]) * inverse
    for copy in w_loads[:W_PIECES]:
        copy.wait()
    for c in (0, 2, 1, 3):
        rs_send[c] = mm(attn[...], w_v[1, :, c * cols : (c + 1) * cols]).astype(BF16)
        x_own(1, c, rs_send.at[c]).start()

    for copy in w_loads[W_PIECES:] + cot_loads:
        copy.wait()
    grad_half(0)
    for way in range(2):
        for i in range(2):
            x_pass(0, way, i).wait_recv()
    grad_half(1)
    for h in range(heads):
        low = ga_t[h * width : (h + 1) * width].astype(BF16)
        do_t[h] = low
        do_s[h] = low.T
        delta[h] = jnp.sum(low.astype(F32) * o_low[h].astype(F32), axis=0, keepdims=True)

    dq_t[...] = jnp.zeros_like(dq_t)

    def bwd_block(stage, d, slot):
        rows = slice(slot * tok, (slot + 1) * tok)
        for h in range(heads):
            prob = exps[d, h] * stage_max[stage, h]
            grad = prob * (mm(kv[d, 1], do_t[h]) - delta[h])
            prob_low[:, h * tok : (h + 1) * tok] = prob.astype(BF16)
            grad_low[rows, h * tok : (h + 1) * tok] = grad.astype(BF16)
        dkv[1] = mm(prob_low[...], do_s[...].reshape(heads * tok, width))
        dkv[0] = mm(grad_low[rows], q_s[...].reshape(heads * tok, width))

    def add_dq(keys_turned, rows):
        for h in range(heads):
            dq_t[h] += mm(keys_turned, grad_low[:rows, h * tok : (h + 1) * tok])

    def part(j):
        return pltpu.make_async_remote_copy(
            src_ref=part_send.at[j - 1], dst_ref=part_recv.at[j - 1],
            send_sem=part_ss.at[j - 1], recv_sem=part_rs.at[j - 1],
            device_id=on(mate, tp), device_id_type=MESH,
        )

    def run(j):
        return pltpu.make_async_remote_copy(
            src_ref=run_send.at[j], dst_ref=run_recv.at[j],
            send_sem=run_ss.at[j], recv_sem=run_rs.at[j],
            device_id=on(prv, tp), device_id_type=MESH,
        )

    def add_part(j):
        part(j).wait_recv()
        dkv[...] += part_recv[j - 1].astype(F32)

    def run_on(j):
        run(j).wait_recv()
        dkv[...] += run_recv[j].astype(F32)

    def backward_step(it, _):
        j = HOPS - it
        bwd_block(j, 2 * j - 1, 0)
        part_send[j - 1] = dkv[...].astype(BF16)
        part(j).start()
        bwd_block(j, 2 * j, 1)
        add_dq(jnp.concatenate([k_t[2 * j - 1], k_t[2 * j]], axis=1), 2 * tok)

        @pl.when((core == 0) & (j < HOPS))
        def _():
            add_part(j + 1)

        @pl.when(core == 1)
        def _():
            add_part(j)

        @pl.when(j < HOPS)
        def _():
            run_on(j)

        run_send[j - 1] = dkv[...].astype(BF16)
        run(j - 1).start()

        @pl.when(j == HOPS)
        def _():
            pass_on(1, 0)

        @pl.when(j == 2)
        def _():
            pass_on(1, 1)

        return 0

    lax.fori_loop(0, HOPS, backward_step, 0)
    bwd_block(0, 0, 0)
    add_dq(k_t[0], tok)
    for h in range(heads):
        dq_out[:, h * width : (h + 1) * width] = (dq_t[h] * score_scale).T.astype(BF16)
    for c in range(CHUNKS):
        own_out[:, c * cols : (c + 1) * cols] = mm(attn[...], w_v[0, :, c * cols : (c + 1) * cols]).astype(BF16)

    @pl.when(core == 0)
    def _():
        add_part(1)

    run_on(0)
    dk_out[...] = (dkv[0] * score_scale).astype(BF16)
    dv_out[...] = dkv[1].astype(BF16)
    for i in range(2):
        for way in range(2):
            c = 2 * way + i
            x_pass(1, way, i).wait_recv()
            at = slice(c * cols, (c + 1) * cols)
            own_out[:, at] = (own_out[:, at].astype(F32) + rs_recv[c].astype(F32)).astype(BF16)

    for j in range(1, HOPS + 1):
        for i in range(2):
            hop(j, i).wait_send()
            from_mate(j, i).wait_send()
        part(j).wait_send()
        run(j - 1).wait_send()
    for ph in range(2):
        for c in range(CHUNKS):
            x_own(ph, c, own_src(ph, c)).wait_send()
            x_pass(ph, c // 2, c % 2).wait_send()


def body(ctx_size, queries, keys, values, out_weight, cotangent, doc_lengths):
    tok = queries.shape[0]
    heads = queries.shape[1] // HEAD_WIDTH
    half = cotangent.shape[1]
    cols = half // CHUNKS
    width = HEAD_WIDTH
    slots = 2 * HOPS + 1
    any_spec = pl.BlockSpec(memory_space=pl.ANY)
    vmem = pltpu.VMEM
    dma = pltpu.SemaphoreType.DMA
    scratch = [
        vmem((heads, tok, width), BF16),
        vmem((heads, width, tok), BF16),
        vmem((slots, 2, tok, width), BF16),
        vmem((slots, width, tok), BF16),
        vmem((width, tok), BF16),
        vmem((width, 2 * tok), BF16),
        vmem((2, heads * width, half), BF16),
        vmem((2, tok, half), BF16),
        vmem((slots, heads, tok, tok), F32),
        vmem((2, tok, tok), F32),
        vmem((heads, width, tok), F32),
        vmem((heads, width, tok), BF16),
        vmem((tok, heads * width), BF16),
        vmem((heads, 1, tok), F32),
        vmem((heads, 1, tok), F32),
        vmem((HOPS + 1, heads, 1, tok), F32),
        vmem((heads, 1, tok), F32),
        vmem((heads * width, tok), F32),
        vmem((heads, width, tok), BF16),
        vmem((heads, tok, width), BF16),
        vmem((heads, width, tok), F32),
        vmem((2, tok, width), F32),
        vmem((HOPS, 2, tok, width), BF16),
        vmem((HOPS, 2, tok, width), BF16),
        vmem((HOPS, 2, tok, width), BF16),
        vmem((HOPS, 2, tok, width), BF16),
        vmem((2, 2, CHUNKS // 2, tok, cols), BF16),
        vmem((CHUNKS, tok, cols), BF16),
        vmem((CHUNKS, tok, cols), BF16),
        vmem((tok, heads * tok), BF16),
        vmem((2 * tok, heads * tok), BF16),
        vmem((2, 2, tok, tok), F32),
        vmem((2, 2 * tok, tok), BF16),
        dma((2 + heads + CHUNKS,)),
        dma((2, W_PIECES)),
        dma((HOPS, 2)), dma((HOPS, 2)),
        dma((HOPS, 2)), dma((HOPS, 2)),
        dma((2, 2, CHUNKS // 2)), dma((2, 2, CHUNKS // 2)),
        dma((2, 2, CHUNKS // 2)), dma((2, 2, CHUNKS // 2)),
        dma((HOPS,)), dma((HOPS,)),
        dma((HOPS,)), dma((HOPS,)),
    ]
    shapes = [(tok, half), (tok, heads * width), (tok, width), (tok, width)]
    results = pl.pallas_call(
        partial(kernel, ctx_size),
        out_shape=tuple(pltpu.VMEM(shape, BF16) for shape in shapes),
        in_specs=[any_spec] * 5 + [pl.BlockSpec(memory_space=pltpu.VMEM)],
        out_specs=[pl.BlockSpec(memory_space=pltpu.VMEM)] * 4,
        scratch_shapes=scratch,
        compiler_params=pltpu.CompilerParams(
            collective_id=0, has_side_effects=True, vmem_limit_bytes=60 * 1024 * 1024
        ),
    )(queries, keys, values, out_weight, cotangent, doc_lengths.reshape(1, -1))
    return pl.pallas_call(
        write_out,
        out_shape=tuple(jax.ShapeDtypeStruct(shape, BF16) for shape in shapes),
        in_specs=[pl.BlockSpec(memory_space=pltpu.VMEM)] * 4,
        out_specs=[any_spec] * 4,
        scratch_shapes=[dma((4,))],
    )(*[pltpu.with_memory_space_constraint(result, pltpu.VMEM) for result in results])


def write_out(*refs):
    sources, targets, sem = refs[:4], refs[4:8], refs[8]
    copies = [pltpu.make_async_copy(a, b, sem.at[i]) for i, (a, b) in enumerate(zip(sources, targets))]
    for copy in copies:
        copy.start()
    for copy in copies:
        copy.wait()


def solution(mesh):
    in_specs = (P("ctx", "tp"), P("ctx", "tp"), P("ctx", "tp"), P("tp", None), P("ctx", "tp"), P())
    out_specs = (P("ctx", "tp"), P("ctx", "tp"), P("ctx", "tp"), P("ctx", "tp"))
    return jax.shard_map(
        partial(body, mesh.shape["ctx"]), mesh=mesh, in_specs=in_specs, out_specs=out_specs, check_vma=False
    )
```
